256 devices in a mesh: grp: 4 (over x), tok: 16 (over z, core), mdl: 4 (over y).
Axes of the slice: x: 4, y: 4, z: 8, core: 2. Of those that a mesh axis runs over, the one named last changes fastest.
Arguments:
- hidden_in: bfloat16 [4, 4096, 2048], P('grp', 'tok', 'mdl'), may hold values from -6 to 6
- suffix_len: int32 [4], P('grp'), may hold values from 512 to 4096, as said below
- norm_gain: bfloat16 [2048], replicated, may hold values from 0.099609375 to 1.8984375
- w_query: bfloat16 [2048, 2048], P(('grp', 'tok'), 'mdl'), may hold values from -0.5 to 0.5
- w_key: bfloat16 [2048, 512], P(('grp', 'tok'), 'mdl'), may hold values from -0.5 to 0.5
- w_value: bfloat16 [2048, 512], P(('grp', 'tok'), 'mdl'), may hold values from -0.125 to 0.125
- w_out: bfloat16 [2048, 2048], P(('grp', 'tok'), 'mdl'), may hold values from -0.5 to 0.5
- sink_logits: float32 [32], P('mdl'), may hold values from 8 to 12
- prefix_keys: bfloat16 [4, 4096, 512], P('grp', 'tok', 'mdl'), may hold values from -280 to 280
- prefix_values: bfloat16 [4, 4096, 512], P('grp', 'tok', 'mdl'), may hold values from -6 to 6
Outputs:
- attn_out: bfloat16 [4, 4096, 2048], P('grp', 'tok', 'mdl')
The draws below stay inside these ranges and needn't reach their ends.
Inputs may be any that keep to these rules, and one draw needn't show every extreme that they name: `suffix_len`: one group in every draw has all 4096 slots live.
All inputs are finite; a program needn't handle non-finite values.
Results may differ from the reference program's by a relative error of at most 0.015.
The reference program's roundings to bfloat16 on the way (of `normed`, `queries`, `weights` and `mixed`) count: a program that leaves them out, or rounds other values in their place, can miss the bound.
Values may be sent and summed in bfloat16 or wider, within the bound.
No kernel may reach another device: no remote copies, remote signals or barrier semaphores. Data moves between devices by JAX's collectives and lax.ppermute only.
A program may use at most 64 MiB of HBM per device.

```python
import jax
import jax.numpy as jnp
from jax import lax

D = 2048
QH = 32
KVH = 8
HD = 64
GROUPS = 4
SUF = 4096
PREFIX = 4096
WINDOW = 4096


def draw_suffix_len(key, part):
    first_key, second_key = jax.random.split(key)
    lengths = jax.random.randint(first_key, (GROUPS,), SUF // 8, SUF + 1)
    chosen = jax.random.randint(second_key, (), 0, GROUPS)
    return jnp.where(jnp.arange(GROUPS) == chosen, SUF, lengths).astype(jnp.int32)


def draw_prefix_keys(key, part):
    shape = (GROUPS, PREFIX, KVH * HD)
    base = 4.0 * jax.random.normal(key, shape, jnp.float32)
    return jnp.clip(base, -24.0, 24.0).astype(jnp.bfloat16)


def block_scale(own_key, dims, cuts, low, high):
    def one(dim, parts):
        steps = jax.random.uniform(jax.random.fold_in(jax.random.fold_in(own_key, 6), dim), (parts,), jnp.float32, low / len(cuts), high / len(cuts))
        return jnp.repeat(jnp.exp(steps), dims[dim] // parts).reshape((-1,) + (1,) * (len(dims) - dim - 1))

    loudness = one(*cuts[0])
    for cut in cuts[1:]:
        loudness = loudness * one(*cut)
    return loudness


def scatter_about(stream_key, extent, scale, limit, pieces=(), held_as=jnp.bfloat16):
    gain = block_scale(stream_key, extent, pieces, -0.22, 0.18) if pieces else 1.0
    values = jax.random.normal(stream_key, extent, jnp.float32) * scale * gain
    return jnp.minimum(jnp.maximum(values, -limit), limit).astype(held_as)


def setup_inputs(seed: int = 0) -> dict:
    streams_of = jax.random.split(jax.random.key(seed), 11)
    return {
        "hidden_in": scatter_about(streams_of[0], (GROUPS, SUF, D), 1.0, 6.0, ((0, 4), (1, 16), (2, 4))),
        "suffix_len": draw_suffix_len(jax.random.fold_in(streams_of[10], 71), 0),
        "norm_gain": jnp.clip(1.0 + 0.18 * jax.random.normal(streams_of[2], (D,), jnp.float32), 0.099609375, 1.8984375).astype(jnp.bfloat16),
        "w_query": scatter_about(streams_of[3], (D, QH * HD), (D // 16) ** -0.5, 0.5, ((0, 64), (1, 4))),
        "w_key": scatter_about(streams_of[4], (D, KVH * HD), (D // 16) ** -0.5, 0.5, ((0, 64), (1, 4))),
        "w_value": scatter_about(streams_of[5], (D, KVH * HD), D ** -0.5, 0.125, ((0, 64), (1, 4))),
        "w_out": scatter_about(streams_of[6], (D, QH * HD), (QH * HD // 16) ** -0.5, 0.5, ((0, 64), (1, 4))),
        "sink_logits": jnp.clip(8.0 + 4.0 * jax.random.uniform(streams_of[7], (QH,), jnp.float32) ** block_scale(streams_of[7], (QH,), ((0, 4),), -0.2, 0.2), 8.0, 12.0),
        "prefix_keys": draw_prefix_keys(jax.random.fold_in(streams_of[10], 71), 0),
        "prefix_values": scatter_about(streams_of[9], (GROUPS, PREFIX, KVH * HD), 1.0, 6.0, ((0, 4), (1, 16), (2, 4))),
    }


SCORE_SCALE = 0.015625
EPSILON = 1e-05
LOG_THETA = 16.11809565095832

def rotate(heads_in, positions):
    half_dim = heads_in.shape[-1] // 2
    frequency = jnp.exp(-LOG_THETA * 2.0 * jnp.arange(half_dim, dtype=jnp.float32) / heads_in.shape[-1])
    angles = positions[:, None] * frequency[None, :]
    cosine = jnp.concatenate([jnp.cos(angles), jnp.cos(angles)], axis=-1)[:, None, :]
    sine_part = jnp.concatenate([jnp.sin(angles), jnp.sin(angles)], axis=-1)[:, None, :]
    turned = jnp.concatenate([-heads_in[..., half_dim:], heads_in[..., :half_dim]], axis=-1)
    return heads_in * cosine + turned * sine_part

def reference(hidden_in, suffix_len, norm_gain, w_query, w_key, w_value, w_out, sink_logits, prefix_keys, prefix_values):
    repeat = QH // KVH
    block_rows = min(512, SUF)
    key_span = WINDOW + block_rows - 1
    sinks = sink_logits.astype(jnp.float32).reshape(KVH, repeat)[:, :, None]

    def one_group(group_args):
        hidden, length, cached_keys, cached_values = group_args
        features = hidden.astype(jnp.float32)
        normed = (features * lax.rsqrt(lax.optimization_barrier(jnp.mean(features * features, axis=-1, keepdims=True)) + EPSILON) * norm_gain.astype(jnp.float32)).astype(jnp.bfloat16)
        positions = (PREFIX + jnp.arange(SUF)).astype(jnp.float32)
        queries = rotate(jnp.dot(normed, w_query, preferred_element_type=jnp.float32).reshape(SUF, QH, HD), positions).astype(jnp.bfloat16)
        new_keys = rotate(jnp.dot(normed, w_key, preferred_element_type=jnp.float32).reshape(SUF, KVH, HD), positions).astype(jnp.bfloat16).reshape(SUF, KVH * HD)
        new_values = jnp.dot(normed, w_value, preferred_element_type=jnp.float32).astype(jnp.bfloat16)
        padding = jnp.zeros((WINDOW, KVH * HD), jnp.bfloat16)
        all_keys = jnp.concatenate([padding, cached_keys, new_keys], axis=0)
        all_values = jnp.concatenate([padding, cached_values, new_values], axis=0)

        def one_block(first_row):
            query_rows = lax.dynamic_slice_in_dim(queries, first_row, block_rows, 0).astype(jnp.float32)
            query_rows = query_rows.reshape(block_rows, KVH, repeat, HD)
            key_rows = lax.dynamic_slice_in_dim(all_keys, PREFIX + first_row + 1, key_span, 0)
            key_rows = key_rows.astype(jnp.float32).reshape(key_span, KVH, HD)
            value_rows = lax.dynamic_slice_in_dim(all_values, PREFIX + first_row + 1, key_span, 0)
            value_rows = value_rows.astype(jnp.float32).reshape(key_span, KVH, HD)
            query_pos = PREFIX + first_row + jnp.arange(block_rows, dtype=jnp.int32)
            key_pos = PREFIX + first_row + 1 - WINDOW + jnp.arange(key_span, dtype=jnp.int32)
            allowed = (key_pos[None, :] <= query_pos[:, None]) & (key_pos[None, :] > query_pos[:, None] - WINDOW) & (key_pos[None, :] >= 0)
            scores = jnp.einsum('bkrh,skh->krbs', query_rows, key_rows) * SCORE_SCALE
            scores = jnp.where(allowed, scores, -jnp.inf)
            row_top = jnp.maximum(lax.optimization_barrier(jnp.max(scores, axis=-1)), sinks)
            expo_terms = jnp.where(allowed, jnp.exp(scores - row_top[..., None]), 0.0)
            denoms = jnp.exp(sinks - row_top) + lax.optimization_barrier(jnp.sum(expo_terms, axis=-1))
            weights = expo_terms.astype(jnp.bfloat16).astype(jnp.float32)
            mixed = jnp.einsum('krbs,skh->krbh', weights, value_rows) / denoms[..., None]
            return jnp.transpose(mixed, (2, 0, 1, 3)).reshape(block_rows, QH * HD)
        starts = jnp.arange(0, SUF, block_rows, dtype=jnp.int32)
        mixed = lax.map(one_block, starts).reshape(SUF, QH * HD)
        live = jnp.arange(SUF, dtype=jnp.int32) < length
        mixed = jnp.where(live[:, None], mixed, 0.0).astype(jnp.bfloat16)
        return jnp.dot(mixed, w_out.T, preferred_element_type=jnp.float32).astype(jnp.bfloat16)
    return lax.map(one_group, (hidden_in, suffix_len, prefix_keys, prefix_values))
```

```python
import functools

import jax
import jax.numpy as jnp
from jax import lax
from jax.experimental import pallas as pl
from jax.experimental.pallas import tpu as pltpu
from jax.sharding import Mesh
from jax.sharding import PartitionSpec as P

HD = 64
SCORE_SCALE = 0.015625
EPSILON = 1e-05
LOG_THETA = 16.11809565095832
LOG2E = 1.4426950408889634
BF16 = jnp.bfloat16
F32 = jnp.float32
VMEM_LIMIT = 50 * 1024 * 1024

NT = (((1,), (1,)), ((), ()))


def params(semantics=None):
    return pltpu.CompilerParams(vmem_limit_bytes=VMEM_LIMIT, dimension_semantics=semantics)


def vspec():
    return pl.BlockSpec(memory_space=pltpu.VMEM)


def sspec():
    return pl.BlockSpec(memory_space=pltpu.SMEM)


def half_turn(x):
    width = x.shape[1]
    lane = lax.broadcasted_iota(jnp.int32, x.shape, 1) % HD
    up = pltpu.roll(x, width - HD // 2, 1)
    down = pltpu.roll(x, HD // 2, 1)
    return jnp.where(lane < HD // 2, -up, down)


def kv_kernel(ids, *refs):
    hid = refs[0:8]
    wts = refs[8:12]
    gain, cos, sin, prefix, normed, own_new, send = refs[12:]
    mdl, grp, zed = ids[0], ids[1], ids[2]
    rows, cols = hid[0].shape
    count = 4
    for side in range(2):
        total = jnp.zeros((rows, 1), F32)
        for k in range(count):
            part = hid[side * count + k][...].astype(F32)
            total = total + jnp.sum(part * part, axis=1, keepdims=True)
        scale = lax.rsqrt(total / (cols * count) + EPSILON)
        for k in range(count):
            at = pl.multiple_of(lax.rem(mdl + k, count) * cols, cols)
            part = hid[side * count + k][...].astype(F32)
            part = part * scale * gain[:, pl.ds(at, cols)].astype(F32)
            normed[side * rows : (side + 1) * rows, pl.ds(at, cols)] = part.astype(BF16)
    depth = wts[0].shape[0]
    acc = None
    for k in range(4):
        at = pl.multiple_of(lax.rem(grp + k, 4) * depth, depth)
        part = jnp.dot(normed[:, pl.ds(at, depth)], wts[k][...], preferred_element_type=F32)
        acc = part if acc is None else acc + part
    lane = lax.broadcasted_iota(jnp.int32, acc.shape, 1)
    turned = acc * cos[...] + half_turn(acc) * sin[...]
    own = jnp.where(lane < HD, turned, acc).astype(BF16)
    own_new[...] = own
    for d in range(send.shape[0]):
        send[d] = jnp.where(zed > d, prefix[...].astype(F32), own.astype(F32)).astype(BF16)


def q_kernel(ids, normed, w0, w1, w2, w3, cos, sin, out):
    grp = ids[1]
    depth = w0.shape[0]
    acc = None
    for k, w in enumerate((w0, w1, w2, w3)):
        at = pl.multiple_of(lax.rem(grp + k, 4) * depth, depth)
        part = jnp.dot(normed[:, pl.ds(at, depth)], w[...], preferred_element_type=F32)
        acc = part if acc is None else acc + part
    turned = half_turn(acc)
    lane = lax.broadcasted_iota(jnp.int32, (acc.shape[0], 2 * HD), 1)
    for pair in range(2):
        cut = slice(pair * 2 * HD, (pair + 1) * 2 * HD)
        both = acc[:, cut] * cos[...] + turned[:, cut] * sin[...]
        both = both.astype(BF16).astype(F32) * SCORE_SCALE
        out[2 * pair] = jnp.where(lane < HD, both, 0.0).astype(BF16)
        out[2 * pair + 1] = jnp.where(lane < HD, pltpu.roll(both, HD, 1), 0.0).astype(BF16)


def attn_kernel(ids, sinks, q, own_prefix, own_new, recv, out, vals):
    zed, core, length = ids[2], ids[3], ids[4]
    half, pair = pl.program_id(0), pl.program_id(1)
    slots, block, _ = recv.shape
    rows = q.shape[1]
    lane = lax.broadcasted_iota(jnp.int32, (block, 2 * HD), 1)

    @pl.when((half == 0) & (pair == 0))
    def _():
        for j in range(slots - 1):
            src = lax.rem(zed + 1 + j, slots)
            vals[j] = jnp.where(lane < HD, 1.0, recv[src].astype(F32)).astype(BF16)
        vals[slots - 1] = jnp.where(lane < HD, 1.0, own_prefix[...].astype(F32)).astype(BF16)
        vals[slots] = jnp.where(lane < HD, 1.0, own_new[...].astype(F32)).astype(BF16)

    row = lax.broadcasted_iota(jnp.int32, (rows, block), 0) + half * rows
    col = lax.broadcasted_iota(jnp.int32, (rows, block), 1)
    swing = core * (block // 2)
    row_pos = lax.rem(row + swing, block)
    col_pos = lax.rem(col + swing, block)
    new_side = col_pos <= row_pos
    accs = []
    for i in range(2):
        queries = q[i]
        sink = sinks[core * 4 + pair * 2 + i]
        scores = []
        for j in range(slots - 1):
            src = lax.rem(zed + 1 + j, slots)
            scores.append(lax.dot_general(queries, recv[src], NT, preferred_element_type=F32))
        before = lax.dot_general(queries, own_prefix[...], NT, preferred_element_type=F32)
        after = lax.dot_general(queries, own_new[...], NT, preferred_element_type=F32)
        diagonal = jnp.where(new_side, after, before)
        top = diagonal
        for s in scores:
            top = jnp.maximum(top, s)
        top = jnp.maximum(jnp.max(top, axis=1, keepdims=True), sink)
        shift = top * LOG2E
        acc = jnp.zeros((rows, 2 * HD), F32)
        for j, s in enumerate(scores):
            p = jnp.exp2(s * LOG2E - shift).astype(BF16)
            acc = acc + jnp.dot(p, vals[j], preferred_element_type=F32)
        p = jnp.exp2(diagonal * LOG2E - shift)
        acc = acc + jnp.dot(
            jnp.where(new_side, 0.0, p).astype(BF16), vals[slots - 1], preferred_element_type=F32
        )
        acc = acc + jnp.dot(
            jnp.where(new_side, p, 0.0).astype(BF16), vals[slots], preferred_element_type=F32
        )
        lane2 = lax.broadcasted_iota(jnp.int32, acc.shape, 1)
        extra = jnp.exp2(sink * LOG2E - shift)
        accs.append(jnp.where(lane2 < HD, acc + extra, acc))
    first, second = accs
    lane2 = lax.broadcasted_iota(jnp.int32, first.shape, 1)
    low = lane2 < HD
    numer = jnp.where(low, pltpu.roll(first, HD, 1), second)
    denom = jnp.where(low, first, pltpu.roll(second, HD, 1))
    pos = lax.broadcasted_iota(jnp.int32, first.shape, 0) + half * rows
    pos = lax.rem(pos + swing, block) + zed * block
    out[0] = jnp.where(pos < length, numer / denom, 0.0).astype(BF16)


def out_kernel(ids, keep, got, *refs):
    grp, core = ids[1], ids[3]
    mine, theirs, out = refs[0:4], refs[4:8], refs[8]
    for k in range(4):
        part = lax.dot_general(keep[...], mine[k][...], NT, preferred_element_type=F32)
        part = part + lax.dot_general(got[...], theirs[k][...], NT, preferred_element_type=F32)
        out[lax.rem(grp + k, 4)] = part.astype(BF16)


def around(x, axis, size):
    got = {k: lax.ppermute(x, axis, [((i + k) % size, i) for i in range(size)]) for k in (1, 3, 2)}
    return [x, got[1], got[2], got[3]]


def swap(x):
    return lax.ppermute(x, "core", [(0, 1), (1, 0)])


def by_core(core, x, width):
    return jnp.stack([x[:, :width], x[:, width:]])


def on_device(
    hidden_in,
    suffix_len,
    norm_gain,
    w_query,
    w_key,
    w_value,
    w_out,
    sink_logits,
    prefix_keys,
    prefix_values,
):
    grp, zed, core, mdl = (lax.axis_index(a) for a in ("grp", "z", "core", "mdl"))
    zsize = lax.axis_size("z")
    hidden = hidden_in[0]
    tok_rows, feats = hidden.shape
    chip_rows = 2 * tok_rows
    ids = jnp.stack([mdl, grp, zed, core, suffix_len[0]]).astype(jnp.int32)

    w_kv = jnp.concatenate([by_core(core, w_key, HD), by_core(core, w_value, HD)], axis=2)
    w_rest = jnp.concatenate(
        [by_core(core, w_query, 4 * HD), by_core(core, w_out, 4 * HD)], axis=2
    )

    def spread(w):
        full = jnp.broadcast_to(w[None], (zsize,) + w.shape).reshape((2 * zsize,) + w.shape[1:])
        got = lax.all_to_all(full, ("z", "core"), 0, 0, tiled=True)
        return got.reshape(-1, w.shape[2])

    w_kv = around(spread(w_kv), "grp", 4)
    hid = around(hidden, "mdl", 4)
    hid_other = [swap(h) for h in hid]
    w_rest = spread(w_rest)
    w_q = around(w_rest[:, : 4 * HD], "grp", 4)
    w_o = around(w_rest[:, 4 * HD :], "grp", 4)
    w_o_other = [swap(w) for w in w_o]

    heads = jnp.concatenate(
        [by_core(core, prefix_keys[0], HD), by_core(core, prefix_values[0], HD)], axis=2
    )
    mine = jnp.where(core == 0, heads[0], heads[1])
    others = jnp.where(core == 0, heads[1], heads[0])
    prefix = jnp.concatenate([mine, swap(others)], axis=0)

    row = jnp.arange(chip_rows, dtype=jnp.int32)
    slot = lax.rem(row + core * tok_rows, chip_rows) + zed * chip_rows
    position = (slot + zsize * chip_rows).astype(F32)
    frequency = jnp.exp(-LOG_THETA * 2.0 * jnp.arange(HD // 2, dtype=F32) / HD)
    angles = position[:, None] * frequency[None, :]
    cos = jnp.tile(jnp.cos(angles), (1, 4))
    sin = jnp.tile(jnp.sin(angles), (1, 4))

    normed, own_new, send = pl.pallas_call(
        kv_kernel,
        out_shape=(
            jax.ShapeDtypeStruct((chip_rows, 4 * feats), BF16),
            jax.ShapeDtypeStruct((chip_rows, 2 * HD), BF16),
            jax.ShapeDtypeStruct((zsize, chip_rows, 2 * HD), BF16),
        ),
        in_specs=[sspec()] + [vspec()] * 16,
        out_specs=(vspec(),) * 3,
        compiler_params=params(),
        name="kv_proj",
    )(ids, *hid, *hid_other, *w_kv, norm_gain.reshape(1, -1), cos, sin, prefix)
    recv = lax.all_to_all(send, "z", 0, 0)

    q = pl.pallas_call(
        q_kernel,
        out_shape=jax.ShapeDtypeStruct((4, chip_rows, 2 * HD), BF16),
        in_specs=[sspec()] + [vspec()] * 7,
        out_specs=vspec(),
        compiler_params=params(),
        name="q_proj",
    )(ids, normed, *w_q, cos, sin)

    mixed = pl.pallas_call(
        attn_kernel,
        out_shape=jax.ShapeDtypeStruct((2, tok_rows, 4 * HD), BF16),
        grid=(2, 2),
        in_specs=[
            sspec(),
            sspec(),
            pl.BlockSpec((2, tok_rows, 2 * HD), lambda i, j: (j, i, 0)),
            vspec(),
            vspec(),
            vspec(),
        ],
        out_specs=pl.BlockSpec((1, tok_rows, 2 * HD), lambda i, j: (i, 0, j)),
        scratch_shapes=[pltpu.VMEM((zsize + 1, chip_rows, 2 * HD), BF16)],
        compiler_params=params(("arbitrary", "arbitrary")),
        name="attention",
    )(ids, sink_logits, q, prefix, own_new, recv)

    got = swap(mixed[1])
    partial_out = pl.pallas_call(
        out_kernel,
        out_shape=jax.ShapeDtypeStruct((4, tok_rows, feats), BF16),
        in_specs=[sspec()] + [vspec()] * 10,
        out_specs=vspec(),
        compiler_params=params(),
        name="out_proj",
    )(ids, mixed[0], got, *w_o, *w_o_other)
    parts = lax.all_to_all(partial_out, "mdl", 0, 0)
    return jnp.sum(parts.astype(F32), axis=0).astype(BF16)[None]


def solution(mesh):
    groups, toks, mdls = mesh.devices.shape
    cores = Mesh(
        mesh.devices.reshape(groups, toks // 2, 2, mdls), ("grp", "z", "core", "mdl")
    )
    tok = ("z", "core")
    placed = (
        P("grp", tok, "mdl"),
        P("grp"),
        P(),
        P(("grp",) + tok, "mdl"),
        P(("grp",) + tok, "mdl"),
        P(("grp",) + tok, "mdl"),
        P(("grp",) + tok, "mdl"),
        P("mdl"),
        P("grp", tok, "mdl"),
        P("grp", tok, "mdl"),
    )
    return jax.shard_map(
        on_device,
        mesh=cores,
        in_specs=placed,
        out_specs=P("grp", tok, "mdl"),
        check_vma=False,
    )
```

```python
import functools

import jax
import jax.numpy as jnp
import numpy as np
from jax import lax
from jax.experimental import pallas as pl
from jax.experimental.pallas import tpu as pltpu
from jax.sharding import Mesh
from jax.sharding import PartitionSpec as P

HD = 64
SCORE_SCALE = 0.015625
EPSILON = 1e-05
LOG_THETA = 16.11809565095832
LOG2E = 1.4426950408889634
BF16 = jnp.bfloat16
F32 = jnp.float32
VMEM_LIMIT = 48 * 1024 * 1024
VMEM_ALL = 63_400_000

AWAY = (1, 7, 2, 6, 3, 5, 4)
NEAR = 4

NT = (((1,), (1,)), ((), ()))


def params(semantics=None, limit=VMEM_LIMIT):
    return pltpu.CompilerParams(vmem_limit_bytes=limit, dimension_semantics=semantics)


def vspec():
    return pl.BlockSpec(memory_space=pltpu.VMEM)


def sspec():
    return pl.BlockSpec(memory_space=pltpu.SMEM)


def half_turn(x):
    width = x.shape[1]
    lane = lax.broadcasted_iota(jnp.int32, x.shape, 1) % HD
    up = pltpu.roll(x, width - HD // 2, 1)
    down = pltpu.roll(x, HD // 2, 1)
    return jnp.where(lane < HD // 2, -up, down)


def rotary_tables(first, step, count):
    frequency = np.exp(-LOG_THETA * 2.0 * np.arange(HD // 2) / HD).astype(np.float32)

    def table(position):
        angles = position[:, None].astype(np.float64) * frequency[None, :].astype(np.float64)
        cos, sin = np.cos(angles), np.sin(angles)
        return np.concatenate([cos, cos, sin, sin], axis=1).astype(np.float32)

    return table(first + step * np.arange(count)), table(np.arange(step))


def split_kernel(ids, wq, wk, wv, wo, pk, pv, fan, p_keep, p_send):
    core = ids[3]

    def halves(*refs):
        low = [r[:, : r.shape[1] // 2] for r in refs]
        high = [r[:, r.shape[1] // 2 :] for r in refs]
        return jnp.concatenate(low, axis=1), jnp.concatenate(high, axis=1)

    for c, half in enumerate(halves(wk, wv, wq, wo)):
        for d in range(fan.shape[0] // 2):
            fan[2 * d + c] = half
    low, high = halves(pk, pv)

    @pl.when(core == 0)
    def _():
        p_keep[...] = low
        p_send[...] = high

    @pl.when(core != 0)
    def _():
        p_keep[...] = high
        p_send[...] = low


def rotary(x, coarse, fine):
    low = lax.broadcasted_iota(jnp.int32, fine.shape, 1) < HD
    low1 = low[:1]

    def pair(t, low):
        other = pltpu.roll(t, HD, 1)
        return jnp.where(low, t, other), jnp.where(low, other, t)

    cos_a, sin_a = pair(coarse, low1)
    cos_b, sin_b = pair(fine, low)
    cos = cos_a * cos_b - sin_a * sin_b
    sin = sin_a * cos_b + cos_a * sin_b
    return x * cos + half_turn(x) * sin


def norm_kernel(ids, *refs):
    hid, gain, normed = refs[0:8], refs[8], refs[9]
    mdl = ids[0]
    rows, cols = hid[0].shape
    count = 4
    for side in range(2):
        total = jnp.zeros((rows, 1), F32)
        for k in range(count):
            part = hid[side * count + k][...].astype(F32)
            total = total + jnp.sum(part * part, axis=1, keepdims=True)
        scale = lax.rsqrt(total / (cols * count) + EPSILON)
        for k in range(count):
            at = pl.multiple_of(lax.rem(mdl + k, count) * cols, cols)
            part = hid[side * count + k][...].astype(F32)
            part = part * scale * gain[:, pl.ds(at, cols)].astype(F32)
            normed[side * rows : (side + 1) * rows, pl.ds(at, cols)] = part.astype(BF16)


def kv_kernel(ids, normed, w0, w1, w2, w3, coarse, fine, p_keep, p_got, own_new, own_prefix, *sends):
    grp, zed, core = ids[1], ids[2], ids[3]
    depth = w0.shape[0]
    rows = p_keep.shape[0]
    acc = None
    for k, w in enumerate((w0, w1, w2, w3)):
        at = pl.multiple_of(lax.rem(grp + k, 4) * depth, depth)
        part = jnp.dot(normed[:, pl.ds(at, depth)], w[...], preferred_element_type=F32)
        acc = part if acc is None else acc + part
    lane = lax.broadcasted_iota(jnp.int32, (rows, 2 * HD), 1)
    turn = coarse[pl.ds(zed, 1), :]
    for side in range(2):
        cut = slice(side * rows, (side + 1) * rows)
        at = pl.multiple_of(lax.rem(side + core, 2) * rows, rows)
        x = acc[cut]
        x = jnp.where(lane < HD, rotary(x, turn, fine[pl.ds(at, rows), :]), x).astype(BF16)
        prefix = (p_keep, p_got)[side][...]
        own_new[cut, :] = x
        own_prefix[cut, :] = prefix
        for away, send in zip(AWAY, sends):
            @pl.when(zed >= away)
            def _(send=send, cut=cut, prefix=prefix):
                send[cut, :] = prefix

            @pl.when(zed < away)
            def _(send=send, cut=cut, x=x):
                send[cut, :] = x


def q_kernel(ids, normed, w0, w1, w2, w3, coarse, fine, q, w_o):
    grp, zed, core = ids[1], ids[2], ids[3]
    depth = w0.shape[0]
    rows = normed.shape[0] // 2
    lane = lax.broadcasted_iota(jnp.int32, (rows, 2 * HD), 1)
    turn = coarse[pl.ds(zed, 1), :]
    weights = (w0, w1, w2, w3)
    for k, w in enumerate(weights):
        w_o[k * depth : (k + 1) * depth, :] = w[:, 4 * HD :]
    for side in range(2):
        cut = slice(side * rows, (side + 1) * rows)
        at = pl.multiple_of(lax.rem(side + core, 2) * rows, rows)
        acc = None
        for k, w in enumerate(weights):
            cols = pl.ds(pl.multiple_of(lax.rem(grp + k, 4) * depth, depth), depth)
            part = jnp.dot(normed[cut, cols], w[:, : 4 * HD], preferred_element_type=F32)
            acc = part if acc is None else acc + part
        for pair in range(2):
            both = rotary(
                acc[:, pair * 2 * HD : (pair + 1) * 2 * HD], turn, fine[pl.ds(at, rows), :]
            )
            both = both.astype(BF16).astype(F32) * SCORE_SCALE
            q[2 * pair, cut, :] = jnp.where(lane < HD, both, 0.0).astype(BF16)
            q[2 * pair + 1, cut, :] = jnp.where(
                lane < HD, pltpu.roll(both, HD, 1), 0.0
            ).astype(BF16)


def ones_and_values(block):
    lane = lax.broadcasted_iota(jnp.int32, block.shape, 1)
    return jnp.where(lane < HD, 1.0, block[...].astype(F32)).astype(BF16)


def attend(scores, top, acc, vals):
    shift = top * LOG2E
    for s, v in zip(scores, vals):
        p = jnp.exp2(s * LOG2E - shift).astype(BF16)
        acc = acc + jnp.dot(p, v[...], preferred_element_type=F32)
    return acc


def first_kernel(ids, sinks, q, own_prefix, own_new, *refs):
    count = len(AWAY[:NEAR])
    blocks, (state, vals) = refs[:count], refs[count:]
    core = ids[3]
    half, pair = pl.program_id(0), pl.program_id(1)
    block, rows = own_new.shape[0], q.shape[1]

    @pl.when((half == 0) & (pair == 0))
    def _():
        for j, b in enumerate((own_prefix, own_new) + tuple(blocks)):
            vals[j] = ones_and_values(b)

    row = lax.broadcasted_iota(jnp.int32, (rows, block), 0) + half * rows
    col = lax.broadcasted_iota(jnp.int32, (rows, block), 1)
    swing = core * (block // 2)
    new_side = lax.rem(col + swing, block) <= lax.rem(row + swing, block)
    for i in range(2):
        queries = q[i]
        sink = sinks[core * 4 + pair * 2 + i]
        scores = [
            lax.dot_general(queries, b[...], NT, preferred_element_type=F32) for b in blocks
        ]
        before = lax.dot_general(queries, own_prefix[...], NT, preferred_element_type=F32)
        after = lax.dot_general(queries, own_new[...], NT, preferred_element_type=F32)
        diagonal = jnp.where(new_side, after, before)
        top = diagonal
        for s in scores:
            top = jnp.maximum(top, s)
        top = jnp.maximum(jnp.max(top, axis=1, keepdims=True), sink)
        shift = top * LOG2E
        p = jnp.exp2(diagonal * LOG2E - shift)
        acc = jnp.dot(
            jnp.where(new_side, 0.0, p).astype(BF16), vals[0], preferred_element_type=F32
        ) + jnp.dot(jnp.where(new_side, p, 0.0).astype(BF16), vals[1], preferred_element_type=F32)
        acc = attend(scores, top, acc, [vals.at[2 + j] for j in range(count)])
        lane = lax.broadcasted_iota(jnp.int32, acc.shape, 1)
        acc = jnp.where(lane < HD, acc + jnp.exp2(sink * LOG2E - shift), acc)
        state[i] = jnp.where(lane < 1, top, acc)


def update(queries, blocks, vals, acc):
    scores = [lax.dot_general(queries, b[...], NT, preferred_element_type=F32) for b in blocks]
    old = acc[:, :1]
    lane = lax.broadcasted_iota(jnp.int32, acc.shape, 1)
    acc = jnp.where(lane < 1, acc[:, 1:2], acc)
    top = scores[0]
    for s in scores[1:]:
        top = jnp.maximum(top, s)
    top = jnp.maximum(jnp.max(top, axis=1, keepdims=True), old)
    acc = acc * jnp.exp2((old - top) * LOG2E)
    return top, attend(scores, top, acc, vals)


def second_kernel(ids, q, state, *refs):
    count = len(AWAY[NEAR:])
    blocks, (out, vals) = refs[:count], refs[count:]
    zed, core, length = ids[2], ids[3], ids[4]
    half, pair = pl.program_id(0), pl.program_id(1)
    rows = q.shape[1]
    block = blocks[0].shape[0]

    @pl.when((half == 0) & (pair == 0))
    def _():
        for j, b in enumerate(blocks):
            vals[j] = ones_and_values(b)

    done = []
    for i in range(2):
        done.append(update(q[i], blocks, [vals.at[j] for j in range(count)], state[i])[1])
    one, two = done
    low = lax.broadcasted_iota(jnp.int32, one.shape, 1) < HD
    numer = jnp.where(low, pltpu.roll(one, HD, 1), two)
    denom = jnp.where(low, one, pltpu.roll(two, HD, 1))
    pos = lax.broadcasted_iota(jnp.int32, one.shape, 0) + half * rows
    pos = lax.rem(pos + core * (block // 2), block) + zed * block
    out[0] = jnp.where(pos < length, numer / denom, 0.0).astype(BF16)


def out_kernel(ids, keep, got, mine, theirs, *outs):
    mdl, grp = ids[0], ids[1]
    feats = outs[0].shape[1]
    for k in range(4):
        at = pl.ds(pl.multiple_of(lax.rem(mdl + k + 4 - grp, 4) * feats, feats), feats)
        part = lax.dot_general(keep[...], mine[at, :], NT, preferred_element_type=F32)
        part = part + lax.dot_general(got[...], theirs[at, :], NT, preferred_element_type=F32)
        outs[k][...] = part.astype(BF16)


def around(x, axis, size):
    got = {k: lax.ppermute(x, axis, [((i + k) % size, i) for i in range(size)]) for k in (1, 3, 2)}
    return [x, got[1], got[2], got[3]]


def swap(x):
    return lax.ppermute(x, "core", [(0, 1), (1, 0)])


def on_device(
    hidden_in,
    suffix_len,
    norm_gain,
    w_query,
    w_key,
    w_value,
    w_out,
    sink_logits,
    prefix_keys,
    prefix_values,
):
    grp, zed, core, mdl = (lax.axis_index(a) for a in ("grp", "z", "core", "mdl"))
    zsize = lax.axis_size("z")
    hidden = hidden_in[0]
    tok_rows, feats = hidden.shape
    chip_rows = 2 * tok_rows
    ids = jnp.stack([mdl, grp, zed, core, suffix_len[0]]).astype(jnp.int32)

    def shaped(*shape):
        return jax.ShapeDtypeStruct(shape, BF16)

    def call(body, name, outs, *args, scalars=1, limit=VMEM_LIMIT):
        whole = lambda x: pl.BlockSpec(x.shape, lambda i, n=len(x.shape): (0,) * n)
        traffic = sum(x.size * x.dtype.itemsize for x in (*args, *jax.tree.leaves(outs)))
        return pl.pallas_call(
            body,
            out_shape=outs,
            grid=(1,),
            in_specs=[sspec()] * scalars + [whole(x) for x in args[scalars:]],
            out_specs=jax.tree.map(whole, outs),
            compiler_params=params(("arbitrary",), limit),
            cost_estimate=pl.CostEstimate(
                flops=10**9, bytes_accessed=traffic, transcendentals=0
            ),
            name=name,
        )(*args)

    rows_in = w_query.shape[0]
    fan, p_keep, p_send = call(
        split_kernel,
        "split",
        (shaped(2 * zsize, rows_in, 10 * HD),) + (shaped(tok_rows, 2 * HD),) * 2,
        ids, w_query, w_key, w_value, w_out, prefix_keys[0], prefix_values[0],
        limit=VMEM_ALL,
    )
    hid = around(hidden, "mdl", 4)
    p_got = swap(p_send)

    depth = 2 * zsize * rows_in
    w_z = lax.all_to_all(fan, ("z", "core"), 0, 0, tiled=True).reshape(depth, 10 * HD)
    hid_other = [swap(h) for h in hid]
    w_z, *both = lax.optimization_barrier((w_z, *hid, *hid_other))
    hid, hid_other = both[:4], both[4:]
    w_kv = around(w_z[:, : 2 * HD], "grp", 4)
    rest, *w_kv = lax.optimization_barrier((w_z[:, 2 * HD :], *w_kv))
    w_qo = around(rest, "grp", 4)

    tables = rotary_tables(zsize * chip_rows, chip_rows, zsize)

    normed = call(
        norm_kernel,
        "norm",
        shaped(chip_rows, 4 * feats),
        ids, *hid, *hid_other, norm_gain.reshape(1, -1),
        limit=VMEM_ALL,
    )
    own_new, prefix, *sends = call(
        kv_kernel,
        "kv_proj",
        (shaped(chip_rows, 2 * HD),) * (2 + len(AWAY)),
        ids, normed, *w_kv, *tables, p_keep, p_got,
        limit=VMEM_ALL,
    )
    blocks = [
        lax.ppermute(x, "z", [(i, (i + zsize - k) % zsize) for i in range(zsize)])
        for k, x in zip(AWAY, sends)
    ]
    q, w_o = call(
        q_kernel,
        "q_proj",
        (shaped(4, chip_rows, 2 * HD), shaped(4 * depth, 4 * HD)),
        ids, normed, *w_qo, *tables,
    )
    w_theirs = swap(w_o)

    def work(count):
        pairs = count * 4 * chip_rows * chip_rows
        return pl.CostEstimate(flops=1024 * pairs, bytes_accessed=2**22, transcendentals=pairs)

    block_spec = pl.BlockSpec((chip_rows, 2 * HD), lambda i, j: (0, 0))
    heads_spec = pl.BlockSpec((2, tok_rows, 2 * HD), lambda i, j: (j, i, 0))
    state = pl.pallas_call(
        first_kernel,
        out_shape=jax.ShapeDtypeStruct((4, chip_rows, 2 * HD), F32),
        grid=(2, 2),
        in_specs=[sspec(), sspec(), heads_spec] + [block_spec] * (2 + NEAR),
        out_specs=heads_spec,
        scratch_shapes=[pltpu.VMEM((2 + NEAR, chip_rows, 2 * HD), BF16)],
        compiler_params=params(("arbitrary", "arbitrary")),
        cost_estimate=work(2 + NEAR),
        name="attention_near",
    )(ids, sink_logits, q, prefix, own_new, *blocks[:NEAR])
    mixed = pl.pallas_call(
        second_kernel,
        out_shape=jax.ShapeDtypeStruct((2, tok_rows, 4 * HD), BF16),
        grid=(2, 2),
        in_specs=[sspec()] + [heads_spec] * 2 + [block_spec] * (len(AWAY) - NEAR),
        out_specs=pl.BlockSpec((1, tok_rows, 2 * HD), lambda i, j: (i, 0, j)),
        scratch_shapes=[pltpu.VMEM((len(AWAY) - NEAR, chip_rows, 2 * HD), BF16)],
        compiler_params=params(("arbitrary", "arbitrary")),
        cost_estimate=work(len(AWAY) - NEAR),
        name="attention_far",
    )(ids, q, state, *blocks[NEAR:])

    got = swap(mixed[1])
    piece = jax.ShapeDtypeStruct((tok_rows, feats), BF16)
    parts = call(out_kernel, "out_proj", (piece,) * 4, ids, mixed[0], got, w_o, w_theirs)
    arrived = {
        k: lax.ppermute(parts[k], "mdl", [(i, (i + k) % 4) for i in range(4)]) for k in (2, 1, 3)
    }
    total = parts[0].astype(F32) + arrived[1].astype(F32)
    total = total + (arrived[2].astype(F32) + arrived[3].astype(F32))
    return total.astype(BF16)[None]


def solution(mesh):
    groups, toks, mdls = mesh.devices.shape
    cores = Mesh(
        mesh.devices.reshape(groups, toks // 2, 2, mdls), ("grp", "z", "core", "mdl")
    )
    tok = ("z", "core")
    placed = (
        P("grp", tok, "mdl"),
        P("grp"),
        P(),
        P(("grp",) + tok, "mdl"),
        P(("grp",) + tok, "mdl"),
        P(("grp",) + tok, "mdl"),
        P(("grp",) + tok, "mdl"),
        P("mdl"),
        P("grp", tok, "mdl"),
        P("grp", tok, "mdl"),
    )
    return jax.shard_map(
        on_device,
        mesh=cores,
        in_specs=placed,
        out_specs=P("grp", tok, "mdl"),
        check_vma=False,
    )
```

```python
import functools

import jax
import jax.numpy as jnp
import numpy as np
from jax import lax
from jax.experimental import pallas as pl
from jax.experimental.pallas import tpu as pltpu
from jax.sharding import Mesh
from jax.sharding import PartitionSpec as P

HD = 64
SCORE_SCALE = 0.015625
EPSILON = 1e-05
LOG_THETA = 16.11809565095832
LOG2E = 1.4426950408889634
BF16 = jnp.bfloat16
F32 = jnp.float32
VMEM_LIMIT = 48 * 1024 * 1024
VMEM_ALL = 63_400_000

AWAY = (1, 7, 2, 6, 3, 5, 4)
NEAR = 4

NT = (((1,), (1,)), ((), ()))


def params(semantics=None, limit=VMEM_LIMIT):
    return pltpu.CompilerParams(vmem_limit_bytes=limit, dimension_semantics=semantics)


def vspec():
    return pl.BlockSpec(memory_space=pltpu.VMEM)


def sspec():
    return pl.BlockSpec(memory_space=pltpu.SMEM)


def half_turn(x):
    width = x.shape[1]
    lane = lax.broadcasted_iota(jnp.int32, x.shape, 1) % HD
    up = pltpu.roll(x, width - HD // 2, 1)
    down = pltpu.roll(x, HD // 2, 1)
    return jnp.where(lane < HD // 2, -up, down)


def rotary_tables(first, step, count):
    frequency = np.exp(-LOG_THETA * 2.0 * np.arange(HD // 2) / HD).astype(np.float32)

    def table(position):
        angles = position[:, None].astype(np.float64) * frequency[None, :].astype(np.float64)
        cos, sin = np.cos(angles), np.sin(angles)
        return np.concatenate([cos, cos, sin, sin], axis=1).astype(np.float32)

    return table(first + step * np.arange(count)), table(np.arange(step))


def split_kernel(ids, wq, wk, wv, wo, pk, pv, fan, p_keep, p_send):
    core = ids[3]

    def halves(*refs):
        low = [r[:, : r.shape[1] // 2] for r in refs]
        high = [r[:, r.shape[1] // 2 :] for r in refs]
        return jnp.concatenate(low, axis=1), jnp.concatenate(high, axis=1)

    for c, half in enumerate(halves(wk, wv, wq, wo)):
        for d in range(fan.shape[0] // 2):
            fan[2 * d + c] = half
    low, high = halves(pk, pv)

    @pl.when(core == 0)
    def _():
        p_keep[...] = low
        p_send[...] = high

    @pl.when(core != 0)
    def _():
        p_keep[...] = high
        p_send[...] = low


def rotary(x, coarse, fine):
    low = lax.broadcasted_iota(jnp.int32, fine.shape, 1) < HD
    low1 = low[:1]

    def pair(t, low):
        other = pltpu.roll(t, HD, 1)
        return jnp.where(low, t, other), jnp.where(low, other, t)

    cos_a, sin_a = pair(coarse, low1)
    cos_b, sin_b = pair(fine, low)
    cos = cos_a * cos_b - sin_a * sin_b
    sin = sin_a * cos_b + cos_a * sin_b
    return x * cos + half_turn(x) * sin


def norm_kernel(ids, *refs):
    hid, gain, normed = refs[0:8], refs[8], refs[9]
    mdl = ids[0]
    rows, cols = hid[0].shape
    count = 4
    for side in range(2):
        total = jnp.zeros((rows, 1), F32)
        for k in range(count):
            part = hid[side * count + k][...].astype(F32)
            total = total + jnp.sum(part * part, axis=1, keepdims=True)
        scale = lax.rsqrt(total / (cols * count) + EPSILON)
        for k in range(count):
            at = pl.multiple_of(lax.rem(mdl + k, count) * cols, cols)
            part = hid[side * count + k][...].astype(F32)
            part = part * scale * gain[:, pl.ds(at, cols)].astype(F32)
            normed[side * rows : (side + 1) * rows, pl.ds(at, cols)] = part.astype(BF16)


def kv_kernel(ids, normed, w0, w1, w2, w3, coarse, fine, p_keep, p_got, own_new, own_prefix, *sends):
    grp, zed, core = ids[1], ids[2], ids[3]
    depth = w0.shape[0]
    rows = p_keep.shape[0]
    acc = None
    for k, w in enumerate((w0, w1, w2, w3)):
        at = pl.multiple_of(lax.rem(grp + k, 4) * depth, depth)
        part = jnp.dot(normed[:, pl.ds(at, depth)], w[...], preferred_element_type=F32)
        acc = part if acc is None else acc + part
    lane = lax.broadcasted_iota(jnp.int32, (rows, 2 * HD), 1)
    turn = coarse[pl.ds(zed, 1), :]
    for side in range(2):
        cut = slice(side * rows, (side + 1) * rows)
        at = pl.multiple_of(lax.rem(side + core, 2) * rows, rows)
        x = acc[cut]
        x = jnp.where(lane < HD, rotary(x, turn, fine[pl.ds(at, rows), :]), x).astype(BF16)
        prefix = (p_keep, p_got)[side][...]
        own_new[cut, :] = x
        own_prefix[cut, :] = prefix
        for away, send in zip(AWAY, sends):
            @pl.when(zed >= away)
            def _(send=send, cut=cut, prefix=prefix):
                send[cut, :] = prefix

            @pl.when(zed < away)
            def _(send=send, cut=cut, x=x):
                send[cut, :] = x


def q_kernel(ids, normed, w0, w1, w2, w3, coarse, fine, q):
    grp, zed, core = ids[1], ids[2], ids[3]
    depth = w0.shape[0]
    rows = normed.shape[0] // 2
    lane = lax.broadcasted_iota(jnp.int32, (rows, 2 * HD), 1)
    turn = coarse[pl.ds(zed, 1), :]
    for side in range(2):
        cut = slice(side * rows, (side + 1) * rows)
        at = pl.multiple_of(lax.rem(side + core, 2) * rows, rows)
        acc = None
        for k, w in enumerate((w0, w1, w2, w3)):
            cols = pl.ds(pl.multiple_of(lax.rem(grp + k, 4) * depth, depth), depth)
            part = jnp.dot(normed[cut, cols], w[...], preferred_element_type=F32)
            acc = part if acc is None else acc + part
        for pair in range(2):
            both = rotary(
                acc[:, pair * 2 * HD : (pair + 1) * 2 * HD], turn, fine[pl.ds(at, rows), :]
            )
            both = both.astype(BF16).astype(F32) * SCORE_SCALE
            q[2 * pair, cut, :] = jnp.where(lane < HD, both, 0.0).astype(BF16)
            q[2 * pair + 1, cut, :] = jnp.where(
                lane < HD, pltpu.roll(both, HD, 1), 0.0
            ).astype(BF16)


def ones_and_values(block):
    lane = lax.broadcasted_iota(jnp.int32, block.shape, 1)
    return jnp.where(lane < HD, 1.0, block[...].astype(F32)).astype(BF16)


def attend(scores, top, acc, vals):
    shift = top * LOG2E
    for s, v in zip(scores, vals):
        p = jnp.exp2(s * LOG2E - shift).astype(BF16)
        acc = acc + jnp.dot(p, v[...], preferred_element_type=F32)
    return acc


def first_kernel(ids, sinks, q, own_prefix, own_new, *refs):
    count = len(AWAY[:NEAR])
    blocks, (state, vals) = refs[:count], refs[count:]
    core = ids[3]
    half, pair = pl.program_id(0), pl.program_id(1)
    block, rows = own_new.shape[0], q.shape[1]

    @pl.when((half == 0) & (pair == 0))
    def _():
        for j, b in enumerate((own_prefix, own_new) + tuple(blocks)):
            vals[j] = ones_and_values(b)

    row = lax.broadcasted_iota(jnp.int32, (rows, block), 0) + half * rows
    col = lax.broadcasted_iota(jnp.int32, (rows, block), 1)
    swing = core * (block // 2)
    new_side = lax.rem(col + swing, block) <= lax.rem(row + swing, block)
    for i in range(2):
        queries = q[i]
        sink = sinks[core * 4 + pair * 2 + i]
        scores = [
            lax.dot_general(queries, b[...], NT, preferred_element_type=F32) for b in blocks
        ]
        before = lax.dot_general(queries, own_prefix[...], NT, preferred_element_type=F32)
        after = lax.dot_general(queries, own_new[...], NT, preferred_element_type=F32)
        diagonal = jnp.where(new_side, after, before)
        top = diagonal
        for s in scores:
            top = jnp.maximum(top, s)
        top = jnp.maximum(jnp.max(top, axis=1, keepdims=True), sink)
        shift = top * LOG2E
        p = jnp.exp2(diagonal * LOG2E - shift)
        acc = jnp.dot(
            jnp.where(new_side, 0.0, p).astype(BF16), vals[0], preferred_element_type=F32
        ) + jnp.dot(jnp.where(new_side, p, 0.0).astype(BF16), vals[1], preferred_element_type=F32)
        acc = attend(scores, top, acc, [vals.at[2 + j] for j in range(count)])
        lane = lax.broadcasted_iota(jnp.int32, acc.shape, 1)
        acc = jnp.where(lane < HD, acc + jnp.exp2(sink * LOG2E - shift), acc)
        state[i] = jnp.where(lane < 1, top, acc)


def update(queries, blocks, vals, acc):
    scores = [lax.dot_general(queries, b[...], NT, preferred_element_type=F32) for b in blocks]
    old = acc[:, :1]
    lane = lax.broadcasted_iota(jnp.int32, acc.shape, 1)
    acc = jnp.where(lane < 1, acc[:, 1:2], acc)
    top = scores[0]
    for s in scores[1:]:
        top = jnp.maximum(top, s)
    top = jnp.maximum(jnp.max(top, axis=1, keepdims=True), old)
    acc = acc * jnp.exp2((old - top) * LOG2E)
    return top, attend(scores, top, acc, vals)


def second_kernel(ids, q, state, *refs):
    count = len(AWAY[NEAR:])
    blocks, (out, vals) = refs[:count], refs[count:]
    zed, core, length = ids[2], ids[3], ids[4]
    half, pair = pl.program_id(0), pl.program_id(1)
    rows = q.shape[1]
    block = blocks[0].shape[0]

    @pl.when((half == 0) & (pair == 0))
    def _():
        for j, b in enumerate(blocks):
            vals[j] = ones_and_values(b)

    done = []
    for i in range(2):
        done.append(update(q[i], blocks, [vals.at[j] for j in range(count)], state[i])[1])
    one, two = done
    low = lax.broadcasted_iota(jnp.int32, one.shape, 1) < HD
    numer = jnp.where(low, pltpu.roll(one, HD, 1), two)
    denom = jnp.where(low, one, pltpu.roll(two, HD, 1))
    pos = lax.broadcasted_iota(jnp.int32, one.shape, 0) + half * rows
    pos = lax.rem(pos + core * (block // 2), block) + zed * block
    out[0] = jnp.where(pos < length, numer / denom, 0.0).astype(BF16)


def out_kernel(ids, keep, got, *refs):
    mdl, grp = ids[0], ids[1]
    mine, theirs, outs, held = refs[0:4], refs[4:8], refs[8:12], refs[12]
    for k in range(4):
        part = lax.dot_general(keep[...], mine[k][...], NT, preferred_element_type=F32)
        part = part + lax.dot_general(got[...], theirs[k][...], NT, preferred_element_type=F32)
        held[lax.rem(grp + k + 4 - mdl, 4)] = part.astype(BF16)
    for k in range(4):
        outs[k][...] = held[k]


def around(x, axis, size):
    got = {k: lax.ppermute(x, axis, [((i + k) % size, i) for i in range(size)]) for k in (1, 3, 2)}
    return [x, got[1], got[2], got[3]]


def swap(x):
    return lax.ppermute(x, "core", [(0, 1), (1, 0)])


def on_device(
    hidden_in,
    suffix_len,
    norm_gain,
    w_query,
    w_key,
    w_value,
    w_out,
    sink_logits,
    prefix_keys,
    prefix_values,
):
    grp, zed, core, mdl = (lax.axis_index(a) for a in ("grp", "z", "core", "mdl"))
    zsize = lax.axis_size("z")
    hidden = hidden_in[0]
    tok_rows, feats = hidden.shape
    chip_rows = 2 * tok_rows
    ids = jnp.stack([mdl, grp, zed, core, suffix_len[0]]).astype(jnp.int32)

    def shaped(*shape):
        return jax.ShapeDtypeStruct(shape, BF16)

    def call(body, name, outs, *args, scalars=1, limit=VMEM_LIMIT, scratch=()):
        whole = lambda x: pl.BlockSpec(x.shape, lambda i, n=len(x.shape): (0,) * n)
        traffic = sum(x.size * x.dtype.itemsize for x in (*args, *jax.tree.leaves(outs)))
        return pl.pallas_call(
            body,
            out_shape=outs,
            grid=(1,),
            in_specs=[sspec()] * scalars + [whole(x) for x in args[scalars:]],
            out_specs=jax.tree.map(whole, outs),
            scratch_shapes=scratch,
            compiler_params=params(("arbitrary",), limit),
            cost_estimate=pl.CostEstimate(
                flops=10**9, bytes_accessed=traffic, transcendentals=0
            ),
            name=name,
        )(*args)

    rows_in = w_query.shape[0]
    fan, p_keep, p_send = call(
        split_kernel,
        "split",
        (shaped(2 * zsize, rows_in, 10 * HD),) + (shaped(tok_rows, 2 * HD),) * 2,
        ids, w_query, w_key, w_value, w_out, prefix_keys[0], prefix_values[0],
        limit=VMEM_ALL,
    )
    hid = around(hidden, "mdl", 4)
    p_got = swap(p_send)

    depth = 2 * zsize * rows_in
    w_z = lax.all_to_all(fan, ("z", "core"), 0, 0, tiled=True).reshape(depth, 10 * HD)
    hid_other = [swap(h) for h in hid]
    w_z, *both = lax.optimization_barrier((w_z, *hid, *hid_other))
    hid, hid_other = both[:4], both[4:]
    w_kv = around(w_z[:, : 2 * HD], "grp", 4)

    tables = rotary_tables(zsize * chip_rows, chip_rows, zsize)

    normed = call(
        norm_kernel,
        "norm",
        shaped(chip_rows, 4 * feats),
        ids, *hid, *hid_other, norm_gain.reshape(1, -1),
        limit=VMEM_ALL,
    )
    own_new, prefix, *sends = call(
        kv_kernel,
        "kv_proj",
        (shaped(chip_rows, 2 * HD),) * (2 + len(AWAY)),
        ids, normed, *w_kv, *tables, p_keep, p_got,
        limit=VMEM_ALL,
    )
    blocks = [
        lax.ppermute(x, "z", [(i, (i + zsize - k) % zsize) for i in range(zsize)])
        for k, x in zip(AWAY, sends)
    ]
    w_q, own_new = lax.optimization_barrier((w_z[:, 2 * HD : 6 * HD], own_new))
    w_q = around(w_q, "grp", 4)
    w_q[1], *blocks[:NEAR] = lax.optimization_barrier((w_q[1], *blocks[:NEAR]))
    q = call(
        q_kernel, "q_proj", shaped(4, chip_rows, 2 * HD), ids, normed, *w_q, *tables
    )
    def work(count):
        pairs = count * 4 * chip_rows * chip_rows
        return pl.CostEstimate(flops=1024 * pairs, bytes_accessed=2**22, transcendentals=pairs)

    block_spec = pl.BlockSpec((chip_rows, 2 * HD), lambda i, j: (0, 0))
    heads_spec = pl.BlockSpec((2, tok_rows, 2 * HD), lambda i, j: (j, i, 0))
    state = pl.pallas_call(
        first_kernel,
        out_shape=jax.ShapeDtypeStruct((4, chip_rows, 2 * HD), F32),
        grid=(2, 2),
        in_specs=[sspec(), sspec(), heads_spec] + [block_spec] * (2 + NEAR),
        out_specs=heads_spec,
        scratch_shapes=[pltpu.VMEM((2 + NEAR, chip_rows, 2 * HD), BF16)],
        compiler_params=params(("arbitrary", "arbitrary")),
        cost_estimate=work(2 + NEAR),
        name="attention_near",
    )(ids, sink_logits, q, prefix, own_new, *blocks[:NEAR])
    state, w_o = lax.optimization_barrier((state, w_z[:, 6 * HD :]))
    w_o = around(w_o, "grp", 4)
    mixed = pl.pallas_call(
        second_kernel,
        out_shape=jax.ShapeDtypeStruct((2, tok_rows, 4 * HD), BF16),
        grid=(2, 2),
        in_specs=[sspec()] + [heads_spec] * 2 + [block_spec] * (len(AWAY) - NEAR),
        out_specs=pl.BlockSpec((1, tok_rows, 2 * HD), lambda i, j: (i, 0, j)),
        scratch_shapes=[pltpu.VMEM((len(AWAY) - NEAR, chip_rows, 2 * HD), BF16)],
        compiler_params=params(("arbitrary", "arbitrary")),
        cost_estimate=work(len(AWAY) - NEAR),
        name="attention_far",
    )(ids, q, state, *blocks[NEAR:])

    mixed, *w_o = lax.optimization_barrier((mixed, *w_o))
    got = swap(mixed[1])
    w_theirs = [swap(w) for w in w_o]
    piece = jax.ShapeDtypeStruct((tok_rows, feats), BF16)
    parts = call(
        out_kernel,
        "out_proj",
        (piece,) * 4,
        ids, mixed[0], got, *w_o, *w_theirs,
        scratch=[pltpu.VMEM((4, tok_rows, feats), BF16)],
    )
    arrived = {
        k: lax.ppermute(parts[k], "mdl", [(i, (i + k) % 4) for i in range(4)]) for k in (2, 1, 3)
    }
    total = parts[0].astype(F32) + arrived[1].astype(F32)
    total = total + (arrived[2].astype(F32) + arrived[3].astype(F32))
    return total.astype(BF16)[None]


def solution(mesh):
    groups, toks, mdls = mesh.devices.shape
    cores = Mesh(
        mesh.devices.reshape(groups, toks // 2, 2, mdls), ("grp", "z", "core", "mdl")
    )
    tok = ("z", "core")
    placed = (
        P("grp", tok, "mdl"),
        P("grp"),
        P(),
        P(("grp",) + tok, "mdl"),
        P(("grp",) + tok, "mdl"),
        P(("grp",) + tok, "mdl"),
        P(("grp",) + tok, "mdl"),
        P("mdl"),
        P("grp", tok, "mdl"),
        P("grp", tok, "mdl"),
    )
    return jax.shard_map(
        on_device,
        mesh=cores,
        in_specs=placed,
        out_specs=P("grp", tok, "mdl"),
        check_vma=False,
    )
```

```python
import functools

import jax
import jax.numpy as jnp
import numpy as np
from jax import lax
from jax.experimental import pallas as pl
from jax.experimental.pallas import tpu as pltpu
from jax.sharding import Mesh
from jax.sharding import PartitionSpec as P

HD = 64
SCORE_SCALE = 0.015625
EPSILON = 1e-05
LOG_THETA = 16.11809565095832
LOG2E = 1.4426950408889634
BF16 = jnp.bfloat16
F32 = jnp.float32
VMEM_LIMIT = 48 * 1024 * 1024
VMEM_ALL = 63_400_000

AWAY = (1, 7, 2, 6, 3, 5, 4)
NEAR = 4

NT = (((1,), (1,)), ((), ()))


def params(semantics=None, limit=VMEM_LIMIT):
    return pltpu.CompilerParams(vmem_limit_bytes=limit, dimension_semantics=semantics)


def vspec():
    return pl.BlockSpec(memory_space=pltpu.VMEM)


def sspec():
    return pl.BlockSpec(memory_space=pltpu.SMEM)


def half_turn(x):
    width = x.shape[1]
    lane = lax.broadcasted_iota(jnp.int32, x.shape, 1) % HD
    up = pltpu.roll(x, width - HD // 2, 1)
    down = pltpu.roll(x, HD // 2, 1)
    return jnp.where(lane < HD // 2, -up, down)


def rotary_tables(first, step, count):
    frequency = np.exp(-LOG_THETA * 2.0 * np.arange(HD // 2) / HD).astype(np.float32)

    def table(position):
        angles = position[:, None].astype(np.float64) * frequency[None, :].astype(np.float64)
        cos, sin = np.cos(angles), np.sin(angles)
        return np.concatenate([cos, cos, sin, sin], axis=1).astype(np.float32)

    return table(first + step * np.arange(count)), table(np.arange(step))


def split_kernel(ids, wq, wk, wv, wo, pk, pv, fan, p_keep, p_send):
    core = ids[3]

    def halves(*refs):
        low = [r[:, : r.shape[1] // 2] for r in refs]
        high = [r[:, r.shape[1] // 2 :] for r in refs]
        return jnp.concatenate(low, axis=1), jnp.concatenate(high, axis=1)

    for c, half in enumerate(halves(wk, wv, wq, wo)):
        for d in range(fan.shape[0] // 2):
            fan[2 * d + c] = half
    low, high = halves(pk, pv)

    @pl.when(core == 0)
    def _():
        p_keep[...] = low
        p_send[...] = high

    @pl.when(core != 0)
    def _():
        p_keep[...] = high
        p_send[...] = low


def rotary(x, coarse, fine):
    low = lax.broadcasted_iota(jnp.int32, fine.shape, 1) < HD
    low1 = low[:1]

    def pair(t, low):
        other = pltpu.roll(t, HD, 1)
        return jnp.where(low, t, other), jnp.where(low, other, t)

    cos_a, sin_a = pair(coarse, low1)
    cos_b, sin_b = pair(fine, low)
    cos = cos_a * cos_b - sin_a * sin_b
    sin = sin_a * cos_b + cos_a * sin_b
    return x * cos + half_turn(x) * sin


def norm_kernel(ids, *refs):
    hid, gain, normed = refs[0:8], refs[8], refs[9]
    mdl = ids[0]
    rows, cols = hid[0].shape
    count = 4
    for side in range(2):
        total = jnp.zeros((rows, 1), F32)
        for k in range(count):
            part = hid[side * count + k][...].astype(F32)
            total = total + jnp.sum(part * part, axis=1, keepdims=True)
        scale = lax.rsqrt(total / (cols * count) + EPSILON)
        for k in range(count):
            at = pl.multiple_of(lax.rem(mdl + k, count) * cols, cols)
            part = hid[side * count + k][...].astype(F32)
            part = part * scale * gain[:, pl.ds(at, cols)].astype(F32)
            normed[side * rows : (side + 1) * rows, pl.ds(at, cols)] = part.astype(BF16)


def kv_kernel(ids, normed, w0, w1, w2, w3, coarse, fine, p_keep, p_got, own_new, own_prefix, *sends):
    grp, zed, core = ids[1], ids[2], ids[3]
    side = pl.program_id(0)
    depth = w0.shape[0]
    rows = p_keep.shape[0]
    acc = None
    for k, w in enumerate((w0, w1, w2, w3)):
        at = pl.multiple_of(lax.rem(grp + k, 4) * depth, depth)
        part = jnp.dot(normed[:, pl.ds(at, depth)], w[...], preferred_element_type=F32)
        acc = part if acc is None else acc + part
    lane = lax.broadcasted_iota(jnp.int32, (rows, 2 * HD), 1)
    at = pl.multiple_of(lax.rem(side + core, 2) * rows, rows)
    turned = rotary(acc, coarse[pl.ds(zed, 1), :], fine[pl.ds(at, rows), :])
    x = jnp.where(lane < HD, turned, acc).astype(BF16)
    own_new[...] = x

    @pl.when(side == 0)
    def _():
        own_prefix[...] = p_keep[...]

    @pl.when(side != 0)
    def _():
        own_prefix[...] = p_got[...]

    for away, send in zip(AWAY, sends):
        @pl.when(zed >= away)
        def _(send=send):
            send[...] = own_prefix[...]

        @pl.when(zed < away)
        def _(send=send):
            send[...] = own_new[...]


def q_kernel(ids, normed, w0, w1, w2, w3, coarse, fine, q):
    grp, zed, core = ids[1], ids[2], ids[3]
    depth = w0.shape[0]
    rows = normed.shape[0] // 2
    lane = lax.broadcasted_iota(jnp.int32, (rows, 2 * HD), 1)
    turn = coarse[pl.ds(zed, 1), :]
    for side in range(2):
        cut = slice(side * rows, (side + 1) * rows)
        at = pl.multiple_of(lax.rem(side + core, 2) * rows, rows)
        acc = None
        for k, w in enumerate((w0, w1, w2, w3)):
            cols = pl.ds(pl.multiple_of(lax.rem(grp + k, 4) * depth, depth), depth)
            part = jnp.dot(normed[cut, cols], w[...], preferred_element_type=F32)
            acc = part if acc is None else acc + part
        for pair in range(2):
            both = rotary(
                acc[:, pair * 2 * HD : (pair + 1) * 2 * HD], turn, fine[pl.ds(at, rows), :]
            )
            both = both.astype(BF16).astype(F32) * SCORE_SCALE
            q[2 * pair, cut, :] = jnp.where(lane < HD, both, 0.0).astype(BF16)
            q[2 * pair + 1, cut, :] = jnp.where(
                lane < HD, pltpu.roll(both, HD, 1), 0.0
            ).astype(BF16)


def ones_and_values(block):
    lane = lax.broadcasted_iota(jnp.int32, block.shape, 1)
    return jnp.where(lane < HD, 1.0, block[...].astype(F32)).astype(BF16)


def attend(scores, top, acc, vals):
    shift = top * LOG2E
    for s, v in zip(scores, vals):
        p = jnp.exp2(s * LOG2E - shift).astype(BF16)
        acc = acc + jnp.dot(p, v[...], preferred_element_type=F32)
    return acc


def first_kernel(ids, sinks, q, own_prefix, own_new, *refs):
    count = len(AWAY[:NEAR])
    blocks, (state, vals, keys) = refs[:count], refs[count:]
    core = ids[3]
    half, pair = pl.program_id(0), pl.program_id(1)
    block, rows = own_new.shape[0], q.shape[1]

    @pl.when((half == 0) & (pair == 0))
    def _():
        for j, b in enumerate((own_prefix, own_new) + tuple(blocks)):
            vals[j] = ones_and_values(b)
        keys[0] = own_prefix[...]
        keys[1] = own_new[...]

    row = lax.broadcasted_iota(jnp.int32, (rows, rows), 0)
    col = lax.broadcasted_iota(jnp.int32, (rows, rows), 1)
    new_side = col <= row
    same = pl.ds(pl.multiple_of(half * rows, rows), rows)
    rest = pl.ds(pl.multiple_of((1 - half) * rows, rows), rows)
    later = lax.rem(half + core, 2)
    for i in range(2):
        queries = q[i]
        sink = sinks[core * 4 + pair * 2 + i]
        scores = [
            lax.dot_general(queries, b[...], NT, preferred_element_type=F32) for b in blocks
        ]
        before = lax.dot_general(queries, own_prefix[same, :], NT, preferred_element_type=F32)
        after = lax.dot_general(queries, own_new[same, :], NT, preferred_element_type=F32)
        diagonal = jnp.where(new_side, after, before)
        across = lax.dot_general(queries, keys[later, rest, :], NT, preferred_element_type=F32)
        top = jnp.maximum(diagonal, across)
        for s in scores:
            top = jnp.maximum(top, jnp.maximum(s[:, :rows], s[:, rows:]))
        top = jnp.maximum(jnp.max(top, axis=1, keepdims=True), sink)
        shift = top * LOG2E
        p = jnp.exp2(diagonal * LOG2E - shift)
        acc = jnp.dot(
            jnp.where(new_side, 0.0, p).astype(BF16), vals[0, same, :], preferred_element_type=F32
        ) + jnp.dot(
            jnp.where(new_side, p, 0.0).astype(BF16), vals[1, same, :], preferred_element_type=F32
        )
        acc = acc + jnp.dot(
            jnp.exp2(across * LOG2E - shift).astype(BF16),
            vals[later, rest, :],
            preferred_element_type=F32,
        )
        acc = attend(scores, top, acc, [vals.at[2 + j] for j in range(count)])
        lane = lax.broadcasted_iota(jnp.int32, acc.shape, 1)
        acc = jnp.where(lane < HD, acc + jnp.exp2(sink * LOG2E - shift), acc)
        state[i] = jnp.where(lane < 1, top, acc)


def update(queries, blocks, vals, acc):
    scores = [lax.dot_general(queries, b[...], NT, preferred_element_type=F32) for b in blocks]
    old = acc[:, :1]
    lane = lax.broadcasted_iota(jnp.int32, acc.shape, 1)
    acc = jnp.where(lane < 1, acc[:, 1:2], acc)
    top = scores[0]
    for s in scores[1:]:
        top = jnp.maximum(top, s)
    top = jnp.maximum(jnp.max(top, axis=1, keepdims=True), old)
    acc = acc * jnp.exp2((old - top) * LOG2E)
    return top, attend(scores, top, acc, vals)


def second_kernel(ids, q, state, *refs):
    count = len(AWAY[NEAR:])
    blocks, (out, vals) = refs[:count], refs[count:]
    zed, core, length = ids[2], ids[3], ids[4]
    half, pair = pl.program_id(0), pl.program_id(1)
    rows = q.shape[1]
    block = blocks[0].shape[0]

    @pl.when((half == 0) & (pair == 0))
    def _():
        for j, b in enumerate(blocks):
            vals[j] = ones_and_values(b)

    done = []
    for i in range(2):
        done.append(update(q[i], blocks, [vals.at[j] for j in range(count)], state[i])[1])
    one, two = done
    low = lax.broadcasted_iota(jnp.int32, one.shape, 1) < HD
    numer = jnp.where(low, pltpu.roll(one, HD, 1), two)
    denom = jnp.where(low, one, pltpu.roll(two, HD, 1))
    pos = lax.broadcasted_iota(jnp.int32, one.shape, 0) + half * rows
    pos = lax.rem(pos + core * (block // 2), block) + zed * block
    out[0] = jnp.where(pos < length, numer / denom, 0.0).astype(BF16)


def out_kernel(ids, keep, got, *refs):
    mdl, grp = ids[0], ids[1]
    mine, theirs, outs, held = refs[0:4], refs[4:8], refs[8:12], refs[12]
    for k in range(4):
        part = lax.dot_general(keep[...], mine[k][...], NT, preferred_element_type=F32)
        part = part + lax.dot_general(got[...], theirs[k][...], NT, preferred_element_type=F32)
        held[lax.rem(grp + k + 4 - mdl, 4)] = part.astype(BF16)
    for k in range(4):
        outs[k][...] = held[k]


def around(x, axis, size):
    got = {k: lax.ppermute(x, axis, [((i + k) % size, i) for i in range(size)]) for k in (1, 3, 2)}
    return [x, got[1], got[2], got[3]]


def swap(x):
    return lax.ppermute(x, "core", [(0, 1), (1, 0)])


def on_device(
    hidden_in,
    suffix_len,
    norm_gain,
    w_query,
    w_key,
    w_value,
    w_out,
    sink_logits,
    prefix_keys,
    prefix_values,
):
    grp, zed, core, mdl = (lax.axis_index(a) for a in ("grp", "z", "core", "mdl"))
    zsize = lax.axis_size("z")
    hidden = hidden_in[0]
    tok_rows, feats = hidden.shape
    chip_rows = 2 * tok_rows
    ids = jnp.stack([mdl, grp, zed, core, suffix_len[0]]).astype(jnp.int32)

    def shaped(*shape):
        return jax.ShapeDtypeStruct(shape, BF16)

    def call(body, name, outs, *args, scalars=1, limit=VMEM_LIMIT, scratch=()):
        whole = lambda x: pl.BlockSpec(x.shape, lambda i, n=len(x.shape): (0,) * n)
        traffic = sum(x.size * x.dtype.itemsize for x in (*args, *jax.tree.leaves(outs)))
        return pl.pallas_call(
            body,
            out_shape=outs,
            grid=(1,),
            in_specs=[sspec()] * scalars + [whole(x) for x in args[scalars:]],
            out_specs=jax.tree.map(whole, outs),
            scratch_shapes=scratch,
            compiler_params=params(("arbitrary",), limit),
            cost_estimate=pl.CostEstimate(
                flops=10**9, bytes_accessed=traffic, transcendentals=0
            ),
            name=name,
        )(*args)

    rows_in = w_query.shape[0]
    fan, p_keep, p_send = call(
        split_kernel,
        "split",
        (shaped(2 * zsize, rows_in, 10 * HD),) + (shaped(tok_rows, 2 * HD),) * 2,
        ids, w_query, w_key, w_value, w_out, prefix_keys[0], prefix_values[0],
        limit=VMEM_ALL,
    )
    hid = around(hidden, "mdl", 4)
    p_got = swap(p_send)

    depth = 2 * zsize * rows_in
    w_z = lax.all_to_all(fan, ("z", "core"), 0, 0, tiled=True).reshape(depth, 10 * HD)
    w_z, *hid = lax.optimization_barrier((w_z, *hid))
    hid_other = [swap(h) for h in hid]
    w_kv = around(w_z[:, : 2 * HD], "grp", 4)

    tables = rotary_tables(zsize * chip_rows, chip_rows, zsize)

    normed = call(
        norm_kernel,
        "norm",
        shaped(chip_rows, 4 * feats),
        ids, *hid, *hid_other, norm_gain.reshape(1, -1),
        limit=VMEM_ALL,
    )
    kv_args = (normed, *w_kv, *tables, p_keep, p_got)
    half = lambda x: pl.BlockSpec((tok_rows, x.shape[1]), lambda i: (i, 0))
    fixed = lambda x: pl.BlockSpec(x.shape, lambda i: (0, 0))
    own_new, prefix, *sends = pl.pallas_call(
        kv_kernel,
        out_shape=(shaped(chip_rows, 2 * HD),) * (2 + len(AWAY)),
        grid=(2,),
        in_specs=[sspec(), half(normed)] + [fixed(x) for x in kv_args[1:]],
        out_specs=(half(p_keep),) * (2 + len(AWAY)),
        compiler_params=params(("arbitrary",), VMEM_ALL),
        cost_estimate=pl.CostEstimate(
            flops=10**9, bytes_accessed=2**22, transcendentals=0
        ),
        name="kv_proj",
    )(ids, *kv_args)
    blocks = [
        lax.ppermute(x, "z", [(i, (i + zsize - k) % zsize) for i in range(zsize)])
        for k, x in zip(AWAY, sends)
    ]
    w_q, own_new = lax.optimization_barrier((w_z[:, 2 * HD : 6 * HD], own_new))
    w_q = around(w_q, "grp", 4)
    w_q[1], *blocks[:NEAR] = lax.optimization_barrier((w_q[1], *blocks[:NEAR]))
    q = call(
        q_kernel, "q_proj", shaped(4, chip_rows, 2 * HD), ids, normed, *w_q, *tables
    )
    def work(count):
        pairs = count * 4 * chip_rows * chip_rows
        return pl.CostEstimate(flops=1024 * pairs, bytes_accessed=2**22, transcendentals=pairs)

    block_spec = pl.BlockSpec((chip_rows, 2 * HD), lambda i, j: (0, 0))
    heads_spec = pl.BlockSpec((2, tok_rows, 2 * HD), lambda i, j: (j, i, 0))
    state = pl.pallas_call(
        first_kernel,
        out_shape=jax.ShapeDtypeStruct((4, chip_rows, 2 * HD), F32),
        grid=(2, 2),
        in_specs=[sspec(), sspec(), heads_spec] + [block_spec] * (2 + NEAR),
        out_specs=heads_spec,
        scratch_shapes=[
            pltpu.VMEM((2 + NEAR, chip_rows, 2 * HD), BF16),
            pltpu.VMEM((2, chip_rows, 2 * HD), BF16),
        ],
        compiler_params=params(("arbitrary", "arbitrary")),
        cost_estimate=work(2 + NEAR),
        name="attention_near",
    )(ids, sink_logits, q, prefix, own_new, *blocks[:NEAR])
    state, w_o = lax.optimization_barrier((state, w_z[:, 6 * HD :]))
    w_o = around(w_o, "grp", 4)
    mixed = pl.pallas_call(
        second_kernel,
        out_shape=jax.ShapeDtypeStruct((2, tok_rows, 4 * HD), BF16),
        grid=(2, 2),
        in_specs=[sspec()] + [heads_spec] * 2 + [block_spec] * (len(AWAY) - NEAR),
        out_specs=pl.BlockSpec((1, tok_rows, 2 * HD), lambda i, j: (i, 0, j)),
        scratch_shapes=[pltpu.VMEM((len(AWAY) - NEAR, chip_rows, 2 * HD), BF16)],
        compiler_params=params(("arbitrary", "arbitrary")),
        cost_estimate=work(len(AWAY) - NEAR),
        name="attention_far",
    )(ids, q, state, *blocks[NEAR:])

    mixed, *w_o = lax.optimization_barrier((mixed, *w_o))
    got = swap(mixed[1])
    w_theirs = [swap(w) for w in w_o]
    piece = jax.ShapeDtypeStruct((tok_rows, feats), BF16)
    parts = call(
        out_kernel,
        "out_proj",
        (piece,) * 4,
        ids, mixed[0], got, *w_o, *w_theirs,
        scratch=[pltpu.VMEM((4, tok_rows, feats), BF16)],
    )
    arrived = {
        k: lax.ppermute(parts[k], "mdl", [(i, (i + k) % 4) for i in range(4)]) for k in (2, 1, 3)
    }
    total = parts[0].astype(F32) + arrived[1].astype(F32)
    total = total + (arrived[2].astype(F32) + arrived[3].astype(F32))
    return total.astype(BF16)[None]


def solution(mesh):
    groups, toks, mdls = mesh.devices.shape
    cores = Mesh(
        mesh.devices.reshape(groups, toks // 2, 2, mdls), ("grp", "z", "core", "mdl")
    )
    tok = ("z", "core")
    placed = (
        P("grp", tok, "mdl"),
        P("grp"),
        P(),
        P(("grp",) + tok, "mdl"),
        P(("grp",) + tok, "mdl"),
        P(("grp",) + tok, "mdl"),
        P(("grp",) + tok, "mdl"),
        P("mdl"),
        P("grp", tok, "mdl"),
        P("grp", tok, "mdl"),
    )
    return jax.shard_map(
        on_device,
        mesh=cores,
        in_specs=placed,
        out_specs=P("grp", tok, "mdl"),
        check_vma=False,
    )
```

```python
import functools

import jax
import jax.numpy as jnp
import numpy as np
from jax import lax
from jax.experimental import pallas as pl
from jax.experimental.pallas import tpu as pltpu
from jax.sharding import Mesh
from jax.sharding import PartitionSpec as P

HD = 64
SCORE_SCALE = 0.015625
EPSILON = 1e-05
LOG_THETA = 16.11809565095832
LOG2E = 1.4426950408889634
BF16 = jnp.bfloat16
F32 = jnp.float32
VMEM_LIMIT = 48 * 1024 * 1024
VMEM_ALL = 63_400_000

AWAY = (1, 7, 2, 6, 3, 5, 4)
NEAR = 3

NT = (((1,), (1,)), ((), ()))


def params(semantics=None, limit=VMEM_LIMIT):
    return pltpu.CompilerParams(vmem_limit_bytes=limit, dimension_semantics=semantics)


def vspec():
    return pl.BlockSpec(memory_space=pltpu.VMEM)


def sspec():
    return pl.BlockSpec(memory_space=pltpu.SMEM)


def half_turn(x):
    width = x.shape[1]
    lane = lax.broadcasted_iota(jnp.int32, x.shape, 1) % HD
    up = pltpu.roll(x, width - HD // 2, 1)
    down = pltpu.roll(x, HD // 2, 1)
    return jnp.where(lane < HD // 2, -up, down)


def rotary_tables(first, step, count):
    frequency = np.exp(-LOG_THETA * 2.0 * np.arange(HD // 2) / HD).astype(np.float32)

    def table(position):
        angles = position[:, None].astype(np.float64) * frequency[None, :].astype(np.float64)
        cos, sin = np.cos(angles), np.sin(angles)
        return np.concatenate([cos, cos, sin, sin], axis=1).astype(np.float32)

    return table(first + step * np.arange(count)), table(np.arange(step))


def split_kernel(ids, wq, wk, wv, wo, pk, pv, fan, p_keep, p_send):
    core = ids[3]

    def halves(*refs):
        low = [r[:, : r.shape[1] // 2] for r in refs]
        high = [r[:, r.shape[1] // 2 :] for r in refs]
        return jnp.concatenate(low, axis=1), jnp.concatenate(high, axis=1)

    for c, half in enumerate(halves(wk, wv, wq, wo)):
        for d in range(fan.shape[0] // 2):
            fan[2 * d + c] = half
    low, high = halves(pk, pv)

    @pl.when(core == 0)
    def _():
        p_keep[...] = low
        p_send[...] = high

    @pl.when(core != 0)
    def _():
        p_keep[...] = high
        p_send[...] = low


def rotary(x, coarse, fine):
    low = lax.broadcasted_iota(jnp.int32, fine.shape, 1) < HD
    low1 = low[:1]

    def pair(t, low):
        other = pltpu.roll(t, HD, 1)
        return jnp.where(low, t, other), jnp.where(low, other, t)

    cos_a, sin_a = pair(coarse, low1)
    cos_b, sin_b = pair(fine, low)
    cos = cos_a * cos_b - sin_a * sin_b
    sin = sin_a * cos_b + cos_a * sin_b
    return x * cos + half_turn(x) * sin


def norm_kernel(ids, *refs):
    hid, gain, normed = refs[0:8], refs[8], refs[9]
    mdl = ids[0]
    rows, cols = hid[0].shape
    count = 4
    for side in range(2):
        total = jnp.zeros((rows, 1), F32)
        for k in range(count):
            part = hid[side * count + k][...].astype(F32)
            total = total + jnp.sum(part * part, axis=1, keepdims=True)
        scale = lax.rsqrt(total / (cols * count) + EPSILON)
        for k in range(count):
            at = pl.multiple_of(lax.rem(mdl + k, count) * cols, cols)
            part = hid[side * count + k][...].astype(F32)
            part = part * scale * gain[:, pl.ds(at, cols)].astype(F32)
            normed[side * rows : (side + 1) * rows, pl.ds(at, cols)] = part.astype(BF16)


def kv_kernel(ids, normed, w0, w1, w2, w3, coarse, fine, p_keep, p_got, own_new, own_prefix, *sends):
    grp, zed, core = ids[1], ids[2], ids[3]
    side = pl.program_id(0)
    depth = w0.shape[0]
    rows = p_keep.shape[0]
    acc = None
    for k, w in enumerate((w0, w1, w2, w3)):
        at = pl.multiple_of(lax.rem(grp + k, 4) * depth, depth)
        part = jnp.dot(normed[:, pl.ds(at, depth)], w[...], preferred_element_type=F32)
        acc = part if acc is None else acc + part
    lane = lax.broadcasted_iota(jnp.int32, (rows, 2 * HD), 1)
    at = pl.multiple_of(lax.rem(side + core, 2) * rows, rows)
    turned = rotary(acc, coarse[pl.ds(zed, 1), :], fine[pl.ds(at, rows), :])
    x = jnp.where(lane < HD, turned, acc).astype(BF16)
    own_new[...] = x

    @pl.when(side == 0)
    def _():
        own_prefix[...] = p_keep[...]

    @pl.when(side != 0)
    def _():
        own_prefix[...] = p_got[...]

    for away, send in zip(AWAY, sends):
        @pl.when(zed >= away)
        def _(send=send):
            send[...] = own_prefix[...]

        @pl.when(zed < away)
        def _(send=send):
            send[...] = own_new[...]


def q_kernel(ids, normed, w0, w1, w2, w3, coarse, fine, q):
    grp, zed, core = ids[1], ids[2], ids[3]
    depth = w0.shape[0]
    rows = normed.shape[0] // 2
    lane = lax.broadcasted_iota(jnp.int32, (rows, 2 * HD), 1)
    turn = coarse[pl.ds(zed, 1), :]
    for side in range(2):
        cut = slice(side * rows, (side + 1) * rows)
        at = pl.multiple_of(lax.rem(side + core, 2) * rows, rows)
        acc = None
        for k, w in enumerate((w0, w1, w2, w3)):
            cols = pl.ds(pl.multiple_of(lax.rem(grp + k, 4) * depth, depth), depth)
            part = jnp.dot(normed[cut, cols], w[...], preferred_element_type=F32)
            acc = part if acc is None else acc + part
        for pair in range(2):
            both = rotary(
                acc[:, pair * 2 * HD : (pair + 1) * 2 * HD], turn, fine[pl.ds(at, rows), :]
            )
            both = both.astype(BF16).astype(F32) * SCORE_SCALE
            q[2 * pair, cut, :] = jnp.where(lane < HD, both, 0.0).astype(BF16)
            q[2 * pair + 1, cut, :] = jnp.where(
                lane < HD, pltpu.roll(both, HD, 1), 0.0
            ).astype(BF16)


def ones_and_values(block):
    lane = lax.broadcasted_iota(jnp.int32, block.shape, 1)
    return jnp.where(lane < HD, 1.0, block[...].astype(F32)).astype(BF16)


def attend(scores, top, acc, vals):
    shift = top * LOG2E
    for s, v in zip(scores, vals):
        p = jnp.exp2(s * LOG2E - shift).astype(BF16)
        acc = acc + jnp.dot(p, v[...], preferred_element_type=F32)
    return acc


def first_kernel(ids, sinks, q, own_prefix, own_new, *refs):
    count = len(AWAY[:NEAR])
    blocks, (state, vals, keys) = refs[:count], refs[count:]
    core = ids[3]
    half, pair = pl.program_id(0), pl.program_id(1)
    block, rows = own_new.shape[0], q.shape[1]

    @pl.when((half == 0) & (pair == 0))
    def _():
        for j, b in enumerate((own_prefix, own_new) + tuple(blocks)):
            vals[j] = ones_and_values(b)
        keys[0] = own_prefix[...]
        keys[1] = own_new[...]

    row = lax.broadcasted_iota(jnp.int32, (rows, rows), 0)
    col = lax.broadcasted_iota(jnp.int32, (rows, rows), 1)
    new_side = col <= row
    same = pl.ds(pl.multiple_of(half * rows, rows), rows)
    rest = pl.ds(pl.multiple_of((1 - half) * rows, rows), rows)
    later = lax.rem(half + core, 2)
    for i in range(2):
        queries = q[i]
        sink = sinks[core * 4 + pair * 2 + i]
        scores = [
            lax.dot_general(queries, b[...], NT, preferred_element_type=F32) for b in blocks
        ]
        before = lax.dot_general(queries, own_prefix[same, :], NT, preferred_element_type=F32)
        after = lax.dot_general(queries, own_new[same, :], NT, preferred_element_type=F32)
        diagonal = jnp.where(new_side, after, before)
        across = lax.dot_general(queries, keys[later, rest, :], NT, preferred_element_type=F32)
        top = jnp.maximum(diagonal, across)
        for s in scores:
            top = jnp.maximum(top, jnp.maximum(s[:, :rows], s[:, rows:]))
        top = jnp.maximum(jnp.max(top, axis=1, keepdims=True), sink)
        shift = top * LOG2E
        p = jnp.exp2(diagonal * LOG2E - shift)
        acc = jnp.dot(
            jnp.where(new_side, 0.0, p).astype(BF16), vals[0, same, :], preferred_element_type=F32
        ) + jnp.dot(
            jnp.where(new_side, p, 0.0).astype(BF16), vals[1, same, :], preferred_element_type=F32
        )
        acc = acc + jnp.dot(
            jnp.exp2(across * LOG2E - shift).astype(BF16),
            vals[later, rest, :],
            preferred_element_type=F32,
        )
        acc = attend(scores, top, acc, [vals.at[2 + j] for j in range(count)])
        lane = lax.broadcasted_iota(jnp.int32, acc.shape, 1)
        acc = jnp.where(lane < HD, acc + jnp.exp2(sink * LOG2E - shift), acc)
        state[i] = jnp.where(lane < 1, top, acc)


def update(queries, blocks, vals, acc):
    scores = [lax.dot_general(queries, b[...], NT, preferred_element_type=F32) for b in blocks]
    old = acc[:, :1]
    lane = lax.broadcasted_iota(jnp.int32, acc.shape, 1)
    acc = jnp.where(lane < 1, acc[:, 1:2], acc)
    top = scores[0]
    for s in scores[1:]:
        top = jnp.maximum(top, s)
    top = jnp.maximum(jnp.max(top, axis=1, keepdims=True), old)
    acc = acc * jnp.exp2((old - top) * LOG2E)
    return top, attend(scores, top, acc, vals)


def second_kernel(ids, q, state, *refs):
    count = len(AWAY[NEAR:])
    blocks, (out, vals) = refs[:count], refs[count:]
    zed, core, length = ids[2], ids[3], ids[4]
    half, pair = pl.program_id(0), pl.program_id(1)
    rows = q.shape[1]
    block = blocks[0].shape[0]

    @pl.when((half == 0) & (pair == 0))
    def _():
        for j, b in enumerate(blocks):
            vals[j] = ones_and_values(b)

    done = []
    for i in range(2):
        done.append(update(q[i], blocks, [vals.at[j] for j in range(count)], state[i])[1])
    one, two = done
    low = lax.broadcasted_iota(jnp.int32, one.shape, 1) < HD
    numer = jnp.where(low, pltpu.roll(one, HD, 1), two)
    denom = jnp.where(low, one, pltpu.roll(two, HD, 1))
    pos = lax.broadcasted_iota(jnp.int32, one.shape, 0) + half * rows
    pos = lax.rem(pos + core * (block // 2), block) + zed * block
    out[0] = jnp.where(pos < length, numer / denom, 0.0).astype(BF16)


def out_kernel(ids, keep, got, *refs):
    mdl, grp = ids[0], ids[1]
    mine, theirs, outs, held = refs[0:4], refs[4:8], refs[8:12], refs[12]
    for k in range(4):
        part = lax.dot_general(keep[...], mine[k][...], NT, preferred_element_type=F32)
        part = part + lax.dot_general(got[...], theirs[k][...], NT, preferred_element_type=F32)
        held[lax.rem(grp + k + 4 - mdl, 4)] = part.astype(BF16)
    for k in range(4):
        outs[k][...] = held[k]


def around(x, axis, size):
    got = {k: lax.ppermute(x, axis, [((i + k) % size, i) for i in range(size)]) for k in (1, 3, 2)}
    return [x, got[1], got[2], got[3]]


def swap(x):
    return lax.ppermute(x, "core", [(0, 1), (1, 0)])


def on_device(
    hidden_in,
    suffix_len,
    norm_gain,
    w_query,
    w_key,
    w_value,
    w_out,
    sink_logits,
    prefix_keys,
    prefix_values,
):
    grp, zed, core, mdl = (lax.axis_index(a) for a in ("grp", "z", "core", "mdl"))
    zsize = lax.axis_size("z")
    hidden = hidden_in[0]
    tok_rows, feats = hidden.shape
    chip_rows = 2 * tok_rows
    ids = jnp.stack([mdl, grp, zed, core, suffix_len[0]]).astype(jnp.int32)

    def shaped(*shape):
        return jax.ShapeDtypeStruct(shape, BF16)

    def call(body, name, outs, *args, scalars=1, limit=VMEM_LIMIT, scratch=()):
        whole = lambda x: pl.BlockSpec(x.shape, lambda i, n=len(x.shape): (0,) * n)
        traffic = sum(x.size * x.dtype.itemsize for x in (*args, *jax.tree.leaves(outs)))
        return pl.pallas_call(
            body,
            out_shape=outs,
            grid=(1,),
            in_specs=[sspec()] * scalars + [whole(x) for x in args[scalars:]],
            out_specs=jax.tree.map(whole, outs),
            scratch_shapes=scratch,
            compiler_params=params(("arbitrary",), limit),
            cost_estimate=pl.CostEstimate(
                flops=10**9, bytes_accessed=traffic, transcendentals=0
            ),
            name=name,
        )(*args)

    rows_in = w_query.shape[0]
    fan, p_keep, p_send = call(
        split_kernel,
        "split",
        (shaped(2 * zsize, rows_in, 10 * HD),) + (shaped(tok_rows, 2 * HD),) * 2,
        ids, w_query, w_key, w_value, w_out, prefix_keys[0], prefix_values[0],
        limit=VMEM_ALL,
    )
    hid = around(hidden, "mdl", 4)
    p_got = swap(p_send)

    depth = 2 * zsize * rows_in
    w_z = lax.all_to_all(fan, ("z", "core"), 0, 0, tiled=True).reshape(depth, 10 * HD)
    w_z, *hid = lax.optimization_barrier((w_z, *hid))
    hid_other = [swap(h) for h in hid]
    w_kv = around(w_z[:, : 2 * HD], "grp", 4)

    tables = rotary_tables(zsize * chip_rows, chip_rows, zsize)

    normed = call(
        norm_kernel,
        "norm",
        shaped(chip_rows, 4 * feats),
        ids, *hid, *hid_other, norm_gain.reshape(1, -1),
        limit=VMEM_ALL,
    )
    kv_args = (normed, *w_kv, *tables, p_keep, p_got)
    half = lambda x: pl.BlockSpec((tok_rows, x.shape[1]), lambda i: (i, 0))
    fixed = lambda x: pl.BlockSpec(x.shape, lambda i: (0, 0))
    own_new, prefix, *sends = pl.pallas_call(
        kv_kernel,
        out_shape=(shaped(chip_rows, 2 * HD),) * (2 + len(AWAY)),
        grid=(2,),
        in_specs=[sspec(), half(normed)] + [fixed(x) for x in kv_args[1:]],
        out_specs=(half(p_keep),) * (2 + len(AWAY)),
        compiler_params=params(("arbitrary",), VMEM_ALL),
        cost_estimate=pl.CostEstimate(
            flops=10**9, bytes_accessed=2**22, transcendentals=0
        ),
        name="kv_proj",
    )(ids, *kv_args)
    blocks = [
        lax.ppermute(x, "z", [(i, (i + zsize - k) % zsize) for i in range(zsize)])
        for k, x in zip(AWAY, sends)
    ]
    w_q, own_new = lax.optimization_barrier((w_z[:, 2 * HD : 6 * HD], own_new))
    w_q = around(w_q, "grp", 4)
    w_q[1], *blocks[:NEAR] = lax.optimization_barrier((w_q[1], *blocks[:NEAR]))
    q = call(
        q_kernel, "q_proj", shaped(4, chip_rows, 2 * HD), ids, normed, *w_q, *tables
    )
    def work(count):
        pairs = count * 4 * chip_rows * chip_rows
        return pl.CostEstimate(flops=1024 * pairs, bytes_accessed=2**22, transcendentals=pairs)

    block_spec = pl.BlockSpec((chip_rows, 2 * HD), lambda i, j: (0, 0))
    heads_spec = pl.BlockSpec((2, tok_rows, 2 * HD), lambda i, j: (j, i, 0))
    state = pl.pallas_call(
        first_kernel,
        out_shape=jax.ShapeDtypeStruct((4, chip_rows, 2 * HD), F32),
        grid=(2, 2),
        in_specs=[sspec(), sspec(), heads_spec] + [block_spec] * (2 + NEAR),
        out_specs=heads_spec,
        scratch_shapes=[
            pltpu.VMEM((2 + NEAR, chip_rows, 2 * HD), BF16),
            pltpu.VMEM((2, chip_rows, 2 * HD), BF16),
        ],
        compiler_params=params(("arbitrary", "arbitrary")),
        cost_estimate=work(2 + NEAR),
        name="attention_near",
    )(ids, sink_logits, q, prefix, own_new, *blocks[:NEAR])
    state, w_o = lax.optimization_barrier((state, w_z[:, 6 * HD :]))
    w_o = around(w_o, "grp", 4)
    mixed = pl.pallas_call(
        second_kernel,
        out_shape=jax.ShapeDtypeStruct((2, tok_rows, 4 * HD), BF16),
        grid=(2, 2),
        in_specs=[sspec()] + [heads_spec] * 2 + [block_spec] * (len(AWAY) - NEAR),
        out_specs=pl.BlockSpec((1, tok_rows, 2 * HD), lambda i, j: (i, 0, j)),
        scratch_shapes=[pltpu.VMEM((len(AWAY) - NEAR, chip_rows, 2 * HD), BF16)],
        compiler_params=params(("arbitrary", "arbitrary")),
        cost_estimate=work(len(AWAY) - NEAR),
        name="attention_far",
    )(ids, q, state, *blocks[NEAR:])

    mixed, *w_o = lax.optimization_barrier((mixed, *w_o))
    got = swap(mixed[1])
    w_theirs = [swap(w) for w in w_o]
    piece = jax.ShapeDtypeStruct((tok_rows, feats), BF16)
    parts = call(
        out_kernel,
        "out_proj",
        (piece,) * 4,
        ids, mixed[0], got, *w_o, *w_theirs,
        scratch=[pltpu.VMEM((4, tok_rows, feats), BF16)],
    )
    arrived = {
        k: lax.ppermute(parts[k], "mdl", [(i, (i + k) % 4) for i in range(4)]) for k in (2, 1, 3)
    }
    total = parts[0].astype(F32) + arrived[1].astype(F32)
    total = total + (arrived[2].astype(F32) + arrived[3].astype(F32))
    return total.astype(BF16)[None]


def solution(mesh):
    groups, toks, mdls = mesh.devices.shape
    cores = Mesh(
        mesh.devices.reshape(groups, toks // 2, 2, mdls), ("grp", "z", "core", "mdl")
    )
    tok = ("z", "core")
    placed = (
        P("grp", tok, "mdl"),
        P("grp"),
        P(),
        P(("grp",) + tok, "mdl"),
        P(("grp",) + tok, "mdl"),
        P(("grp",) + tok, "mdl"),
        P(("grp",) + tok, "mdl"),
        P("mdl"),
        P("grp", tok, "mdl"),
        P("grp", tok, "mdl"),
    )
    return jax.shard_map(
        on_device,
        mesh=cores,
        in_specs=placed,
        out_specs=P("grp", tok, "mdl"),
        check_vma=False,
    )
```
